32 devices in a mesh: vocab: 4 (over x, core), fsdp: 8 (over z, y).
Axes of the slice: x: 2, y: 2, z: 4, core: 2. Of those that a mesh axis runs over, the one named last changes fastest.
Arguments:
- hidden: bfloat16 [2, 384, 4096], P(None, 'fsdp'), may hold values from -1000 to 1000
- norm_gain: bfloat16 [4096], replicated, may hold values from 0.5 to 1.5
- labels: int32 [2, 384], P(None, 'fsdp'), may hold values from 0 to 65535
- head_weight: bfloat16 [4096, 65536], P(None, ('vocab', 'fsdp')), may hold values from -1 to 1
- head_ema: float32 [4096, 65536], P(None, ('vocab', 'fsdp')), may hold values from 1e-09 to 0.001
- gain_ema: float32 [4096], replicated, may hold values from 0.0001 to 0.03
Outputs:
- head_ema_new: float32 [4096, 65536], P(None, ('vocab', 'fsdp'))
- gain_ema_new: float32 [4096], replicated
The draws below stay inside these ranges and needn't reach their ends.
All inputs are finite; a program needn't handle non-finite values.
Results may differ from the reference program's by a relative error of at most 0.00049.
Values may be sent and summed in bfloat16 or wider, within the bound.
A program may use at most 192 MiB of HBM per device.

```python
import math
import jax
import jax.numpy as jnp
import numpy as np
from jax import lax

D = 4096
V = 65536
MB = 2
TOKENS = 384


def build_pair(key):
    base_key = jax.random.fold_in(key, 7)
    k_weight, k_common, k_noise, k_rows, k_cols = jax.random.split(base_key, 5)
    weight = jax.random.normal(k_weight, (D, V), jnp.float32) * (3.0 / math.sqrt(D))
    noise = jax.random.normal(k_noise, (MB, TOKENS, D), jnp.float32)
    common = jax.random.normal(k_common, (D,), jnp.float32)
    row_scale = jnp.exp(jax.random.uniform(k_rows, (MB, TOKENS, 1), jnp.float32, 0.0, math.log(10.0)))
    col_scale = jnp.exp(jax.random.uniform(k_cols, (D,), jnp.float32, 0.0, math.log(10.0)))
    states = (noise + common[None, None, :]) * row_scale * col_scale[None, None, :]
    limit = 1.0 + 2600 // D
    states = jnp.clip(states, -1000.0, 1000.0)
    weight = jnp.clip(weight, -limit, limit)
    return (states, weight)


def draw_hidden(key, part):
    states, weight = build_pair(key)
    return states.astype(jnp.bfloat16)


def draw_head_weight(key, part):
    states, weight = build_pair(key)
    return weight.astype(jnp.bfloat16)


def set_ends(values, rng, low, largest):
    extent = values.shape
    index_at = [jax.random.randint(jax.random.fold_in(rng, axis), (), 0, extent[axis]) for axis in range(len(extent))]
    values = values.at[tuple(index_at)].set(low)
    longest = extent.index(max(extent))
    index_at[longest] = (index_at[longest] + 1) % extent[longest]
    return values.at[tuple(index_at)].set(largest)


def block_levels(rng, extent, cuts, smallest, top_value):
    level = 1.0
    for position, shards_of in cuts:
        heights = jax.random.uniform(jax.random.fold_in(jax.random.fold_in(rng, 6), position), (shards_of,), jnp.float32, smallest / len(cuts), top_value / len(cuts))
        level = level * jnp.repeat(jnp.exp(heights), extent[position] // shards_of).reshape((-1,) + (1,) * (len(extent) - 1 - position))
    return level


def rank_table(number_of, skew):
    weights = [(1 << 20) // math.isqrt(rank ** skew) + 1 for rank in range(1, number_of + 1)]
    scale = 1 + sum(weights) // (1 << 30)
    return np.cumsum(np.array([max(1, weight // scale) for weight in weights]))


def ranked_ids(own_key, shape, amount, skew):
    grid = rank_table(amount, skew)
    lot = jax.random.randint(jax.random.fold_in(own_key, 1), shape, 0, int(grid[amount - 1]))
    standing = jnp.searchsorted(jnp.asarray(grid, jnp.int32), lot, side="right")
    return jax.random.permutation(jax.random.fold_in(own_key, 2), amount)[standing].astype(jnp.int32)


def setup_inputs(seed: int = 0) -> dict:
    splits = jax.random.split(jax.random.key(seed), 7)
    return {
        "hidden": draw_hidden(jax.random.fold_in(splits[6], 71), 0),
        "norm_gain": jnp.clip(1.0 + 0.1 * jax.random.normal(splits[1], (D,), jnp.float32), 0.5, 1.5).astype(jnp.bfloat16),
        "labels": set_ends(ranked_ids(splits[2], (MB, TOKENS), V, 2), jax.random.fold_in(splits[2], 3), 0, V - 1).astype(jnp.int32),
        "head_weight": draw_head_weight(jax.random.fold_in(splits[6], 71), 0),
        "head_ema": jnp.clip(jnp.exp(math.log(0.001) - 13.815511 * jax.random.uniform(splits[4], (D, V), jnp.float32) ** block_levels(splits[4], (D, V), ((1, 32),), -0.2, 0.2)), 9.999999717180685e-10, 0.001),
        "gain_ema": jnp.clip(jnp.exp(jax.random.uniform(splits[5], (D,), jnp.float32, math.log(0.0001), math.log(0.03))), 0.0001, 0.03),
    }


BETA = 0.99
EPS = 1e-05

def normalize(hidden, norm_gain):
    wide = hidden.astype(jnp.float32)
    factor = lax.rsqrt(lax.optimization_barrier(jnp.mean(wide * wide, axis=-1, keepdims=True)) + EPS)
    return (wide * factor * norm_gain.astype(jnp.float32)).astype(jnp.bfloat16)

def reference(hidden, norm_gain, labels, head_weight, head_ema, gain_ema):
    scaled = normalize(hidden, norm_gain)
    columns = lax.iota(jnp.int32, V)
    gradient = jnp.zeros((D, V), jnp.float32)
    for batch in range(MB):
        logits = jnp.dot(scaled[batch], head_weight, preferred_element_type=jnp.float32)
        row_top = lax.optimization_barrier(jnp.max(logits, axis=1, keepdims=True))
        shifted = jnp.exp(logits - row_top)
        chances = shifted / lax.optimization_barrier(jnp.sum(shifted, axis=1, keepdims=True))
        hits = (labels[batch][:, None] == columns[None, :]).astype(jnp.float32)
        slope = (chances - hits).astype(jnp.bfloat16)
        gradient = gradient + jnp.dot(scaled[batch].T, slope, preferred_element_type=jnp.float32)
    count = MB * TOKENS
    head_new = BETA * head_ema + (1.0 - BETA) * gradient * gradient / count
    gain_grad = lax.optimization_barrier(jnp.sum(head_weight.astype(jnp.float32) * gradient, axis=1)) / norm_gain.astype(jnp.float32)
    gain_new = BETA * gain_ema + (1.0 - BETA) * gain_grad * gain_grad / count
    return (head_new, gain_new)
```

```python
import functools

import jax
import jax.numpy as jnp
from jax import lax
from jax.experimental import pallas as pl
from jax.experimental.pallas import tpu as pltpu
from jax.sharding import PartitionSpec as P

BETA = 0.99
EPS = 1e-05
LANES = 128
MESH = pl.DeviceIdType.MESH
VMEM_LIMIT = 60 * 1024 * 1024


def bits_of(size):
    return [1 << place for place in reversed(range(size.bit_length() - 1))]


def flip(index, mask):
    for place in range(mask.bit_length()):
        bit = 1 << place
        if mask & bit:
            index = index + bit - 2 * bit * lax.rem(lax.div(index, bit), 2)
    return index


def shared_width(features, ways):
    return features // 8 // LANES * LANES if ways == 4 else 0


def gather_sends(parts, ways, features):
    return (parts - 1) * (ways + (2 if shared_width(features, ways) else 0))


def gather_kernel(parts, ways, own_ref, all_ref, send_sem, recv_sem, local_sem):
    part, way = lax.axis_index("fsdp"), lax.axis_index("vocab")
    features = own_ref.shape[1]
    both = shared_width(features, ways)
    single = (features - 2 * both) // ways
    part_bits, way_bits = bits_of(parts), bits_of(ways)

    barrier = pltpu.get_barrier_semaphore()
    for bit in part_bits:
        pl.semaphore_signal(barrier, inc=1, device_id=(way, flip(part, bit)), device_id_type=MESH)
    for bit in way_bits:
        pl.semaphore_signal(barrier, inc=1, device_id=(flip(way, bit), part), device_id_type=MESH)
    pl.semaphore_wait(barrier, len(part_bits) + len(way_bits))

    kinds = ([("both", [1])] if both else []) + [("single", way_bits)]

    def columns(kind, piece_mask):
        piece = flip(way, piece_mask)
        if kind == "both":
            return pl.ds(pl.multiple_of(single * ways + lax.rem(piece, 2) * both, LANES), both)
        return pl.ds(pl.multiple_of(piece * single, LANES), single)

    def slot(kind, part_mask, piece_mask):
        return (part_mask - 1) * (ways + 2) + (ways if kind == "both" else 0) + piece_mask

    sends = []

    def send(kind, part_mask, piece_mask, part_bit, way_bit):
        where = columns(kind, piece_mask)
        shard = flip(part, part_mask)
        target = all_ref.at[shard, :, where]
        copy = pltpu.make_async_remote_copy(
            src_ref=target if part_mask else own_ref.at[:, where],
            dst_ref=target,
            send_sem=send_sem.at[len(sends)],
            recv_sem=recv_sem.at[slot(kind, part_mask ^ part_bit, piece_mask ^ way_bit)],
            device_id=(flip(way, way_bit), flip(part, part_bit)),
            device_id_type=MESH,
        )
        copy.start()
        sends.append(copy)

    def forward(kind, kind_bits, part_mask, piece_mask):
        if not piece_mask:
            for bit in part_bits:
                if not part_mask or bit < part_mask & -part_mask:
                    send(kind, part_mask, 0, bit, 0)
        if part_mask:
            for bit in kind_bits:
                if not piece_mask or bit < piece_mask & -piece_mask:
                    send(kind, part_mask, piece_mask, 0, bit)

    def arrive(kind, part_mask, piece_mask):
        target = all_ref.at[flip(part, part_mask), :, columns(kind, piece_mask)]
        pltpu.make_async_remote_copy(
            src_ref=target,
            dst_ref=target,
            send_sem=send_sem.at[0],
            recv_sem=recv_sem.at[slot(kind, part_mask, piece_mask)],
            device_id=(flip(way, way_bits[-1]), part),
            device_id_type=MESH,
        ).wait_recv()

    keep = pltpu.make_async_copy(own_ref, all_ref.at[part], local_sem)
    for kind, kind_bits in reversed(kinds):
        forward(kind, kind_bits, 0, 0)
    keep.start()
    order = sorted(range(1, parts), key=lambda mask: (mask.bit_count(), -mask))
    for part_mask in order:
        for kind, kind_bits in reversed(kinds):
            arrive(kind, part_mask, 0)
            forward(kind, kind_bits, part_mask, 0)
    for last in (False, True):
        for part_mask in order:
            for kind, kind_bits in reversed(kinds):
                for piece_mask in range(1, 2 * kind_bits[0]):
                    if (piece_mask % 2 == 1) == last:
                        arrive(kind, part_mask, piece_mask)
                        forward(kind, kind_bits, part_mask, piece_mask)
    for copy in sends:
        copy.wait_send()
    keep.wait()


def gather_rows(own, parts, ways):
    rows, features = own.shape
    sends = gather_sends(parts, ways, features)
    return pl.pallas_call(
        functools.partial(gather_kernel, parts, ways),
        out_shape=jax.ShapeDtypeStruct((parts, rows, features), own.dtype),
        in_specs=[pl.BlockSpec(memory_space=pltpu.VMEM)],
        out_specs=pl.BlockSpec(memory_space=pl.ANY),
        scratch_shapes=[
            pltpu.SemaphoreType.DMA((sends,)),
            pltpu.SemaphoreType.DMA(((parts - 1) * (ways + 2),)),
            pltpu.SemaphoreType.DMA,
        ],
        compiler_params=pltpu.CompilerParams(collective_id=0, has_side_effects=True),
        name="gather_rows",
    )(own)


def exchange_kernel(parts, ways, combine, x_ref, y_ref, part_slots, way_slots, half, send_sem, part_sem, way_sem):
    part, way = lax.axis_index("fsdp"), lax.axis_index("vocab")
    barrier = pltpu.get_barrier_semaphore()
    for step in range(1, parts):
        pl.semaphore_signal(barrier, inc=1, device_id=(way, lax.rem(part + step, parts)), device_id_type=MESH)
    for step in range(1, ways):
        pl.semaphore_signal(barrier, inc=1, device_id=(lax.rem(way + step, ways), part), device_id_type=MESH)
    pl.semaphore_wait(barrier, parts + ways - 2)

    copies = []
    for step in range(1, parts):
        copies.append(
            pltpu.make_async_remote_copy(
                src_ref=x_ref,
                dst_ref=part_slots.at[part],
                send_sem=send_sem.at[step - 1],
                recv_sem=part_sem.at[step - 1],
                device_id=(way, lax.rem(part + step, parts)),
                device_id_type=MESH,
            )
        )
        copies[-1].start()
    part_slots[part] = x_ref[...]
    for step in range(1, parts):
        pltpu.make_async_remote_copy(
            src_ref=x_ref,
            dst_ref=part_slots.at[lax.rem(part + parts - step, parts)],
            send_sem=send_sem.at[step - 1],
            recv_sem=part_sem.at[step - 1],
            device_id=(way, lax.rem(part + step, parts)),
            device_id_type=MESH,
        ).wait_recv()
    half[...] = combine([part_slots[index] for index in range(parts)], False)
    for step in range(1, ways):
        copies.append(
            pltpu.make_async_remote_copy(
                src_ref=half,
                dst_ref=way_slots.at[way],
                send_sem=send_sem.at[parts - 2 + step],
                recv_sem=way_sem.at[step - 1],
                device_id=(lax.rem(way + step, ways), part),
                device_id_type=MESH,
            )
        )
        copies[-1].start()
    way_slots[way] = half[...]
    for step in range(1, ways):
        pltpu.make_async_remote_copy(
            src_ref=half,
            dst_ref=way_slots.at[lax.rem(way + ways - step, ways)],
            send_sem=send_sem.at[parts - 2 + step],
            recv_sem=way_sem.at[step - 1],
            device_id=(lax.rem(way + step, ways), part),
            device_id_type=MESH,
        ).wait_recv()
    y_ref[...] = combine([way_slots[index] for index in range(ways)], True)
    for copy in copies:
        copy.wait_send()


def exchange(x, parts, ways, combine, number, name):
    return pl.pallas_call(
        functools.partial(exchange_kernel, parts, ways, combine),
        out_shape=jax.ShapeDtypeStruct(x.shape, x.dtype),
        in_specs=[pl.BlockSpec(memory_space=pltpu.VMEM)],
        out_specs=pl.BlockSpec(memory_space=pltpu.VMEM),
        scratch_shapes=[
            pltpu.VMEM((parts,) + x.shape, x.dtype),
            pltpu.VMEM((ways,) + x.shape, x.dtype),
            pltpu.VMEM(x.shape, x.dtype),
            pltpu.SemaphoreType.DMA((parts + ways - 2,)),
            pltpu.SemaphoreType.DMA((parts - 1,)),
            pltpu.SemaphoreType.DMA((ways - 1,)),
        ],
        compiler_params=pltpu.CompilerParams(collective_id=number, has_side_effects=True),
        name=name,
    )(x)


def combine_stats(terms, labels_done):
    top = functools.reduce(jnp.maximum, [term[0:1] for term in terms])
    total = sum(term[1:2] * jnp.exp(term[0:1] - top) for term in terms)
    label = terms[0][2:3] if labels_done else sum(term[2:3] for term in terms)
    return jnp.concatenate([top, total, label, jnp.zeros((5, top.shape[1]), jnp.float32)], axis=0)


def combine_sum(terms, labels_done):
    return sum(terms)


def logits_kernel(rows_ref, weight_ref, label_ref, logits_ref, stats_ref, top_ref, total_ref):
    step = pl.program_id(0)

    @pl.when(step == 0)
    def _():
        top_ref[...] = jnp.full_like(top_ref, -jnp.inf)
        total_ref[...] = jnp.zeros_like(total_ref)

    logits_ref[...] = jnp.dot(rows_ref[...], weight_ref[...], preferred_element_type=jnp.float32)
    groups = [logits_ref[:, start : start + LANES] for start in range(0, logits_ref.shape[1], LANES)]
    old = top_ref[...]
    top = functools.reduce(jnp.maximum, groups, old)
    total_ref[...] = total_ref[...] * jnp.exp(old - top) + sum(jnp.exp(group - top) for group in groups)
    top_ref[...] = top

    @pl.when(step == pl.num_programs(0) - 1)
    def _():
        wide_top = top_ref[...].T
        row_top = jnp.max(wide_top, axis=0, keepdims=True)
        row_total = jnp.sum(total_ref[...].T * jnp.exp(wide_top - row_top), axis=0, keepdims=True)
        stats_ref[...] = jnp.concatenate(
            [row_top, row_total, label_ref[...], jnp.zeros((5, row_top.shape[1]), jnp.float32)], axis=0
        )


def local_logits(rows_all, head_weight, label_row):
    rows, features = rows_all.shape
    columns = head_weight.shape[1]
    tile = min(256, columns)
    return pl.pallas_call(
        logits_kernel,
        grid=(columns // tile,),
        out_shape=(
            jax.ShapeDtypeStruct((rows, columns), jnp.float32),
            jax.ShapeDtypeStruct((8, rows), jnp.float32),
        ),
        in_specs=[
            pl.BlockSpec((rows, features), lambda i: (0, 0), pipeline_mode=pl.Buffered(1)),
            pl.BlockSpec((features, tile), lambda i: (0, i)),
            pl.BlockSpec((1, rows), lambda i: (0, 0)),
        ],
        out_specs=(pl.BlockSpec((rows, tile), lambda i: (0, i)), pl.BlockSpec((8, rows), lambda i: (0, 0))),
        scratch_shapes=[pltpu.VMEM((rows, LANES), jnp.float32)] * 2,
        compiler_params=pltpu.CompilerParams(vmem_limit_bytes=VMEM_LIMIT),
        name="local_logits",
    )(rows_all, head_weight, label_row)


def update_kernel(
    chunk, rows_ref, stats_ref, logits_ref, weight_ref, ema_ref, new_ref, gain_ref, slope_ref, top_ref, scale_ref, label_ref
):
    count, columns = logits_ref.shape

    @pl.when(pl.program_id(0) == 0)
    def _():
        stats = stats_ref[...]
        top_ref[...] = jnp.broadcast_to(stats[0:1], (LANES, count)).T
        scale_ref[...] = jnp.broadcast_to(1.0 / stats[1:2], (LANES, count)).T
        label_ref[...] = jnp.broadcast_to(stats[2:3], (LANES, count)).T
        first = (lax.axis_index("vocab") * lax.axis_size("fsdp") + lax.axis_index("fsdp")) * columns

        @pl.loop(0, count // chunk)
        def _(index):
            some = pl.ds(pl.multiple_of(index * chunk, chunk), chunk)
            top, scale, label = top_ref[some, :], scale_ref[some, :], label_ref[some, :].astype(jnp.int32)
            label = label - first
            lane = lax.broadcasted_iota(jnp.int32, (chunk, LANES), 1)
            for start in range(0, columns, LANES):
                chances = jnp.exp(logits_ref[some, start : start + LANES] - top) * scale
                hits = (label == lane + start).astype(jnp.float32)
                slope_ref[some, start : start + LANES] = (chances - hits).astype(slope_ref.dtype)

    mix = (1.0 - BETA) / count
    tall = rows_ref[...].T
    total = jnp.zeros((tall.shape[0], LANES), jnp.float32)
    width = min(512, columns)
    for start in range(0, columns, width):
        gradient = jnp.dot(tall, slope_ref[:, start : start + width], preferred_element_type=jnp.float32)
        new_ref[:, start : start + width] = BETA * ema_ref[:, start : start + width] + mix * gradient * gradient
        product = weight_ref[:, start : start + width].astype(jnp.float32) * gradient
        for lane in range(0, width, LANES):
            total = total + product[:, lane : lane + LANES]
    gain_ref[...] = jnp.sum(total.T, axis=0, keepdims=True)


def head_update(rows_all, stats, logits, head_weight, head_ema, chunk):
    rows, features = rows_all.shape
    columns = head_weight.shape[1]
    tile = 256
    once = dict(pipeline_mode=pl.Buffered(1))
    return pl.pallas_call(
        functools.partial(update_kernel, chunk),
        grid=(features // tile,),
        out_shape=(
            jax.ShapeDtypeStruct((features, columns), jnp.float32),
            jax.ShapeDtypeStruct((1, features), jnp.float32),
        ),
        in_specs=[
            pl.BlockSpec((rows, tile), lambda i: (0, i)),
            pl.BlockSpec((8, rows), lambda i: (0, 0)),
            pl.BlockSpec((rows, columns), lambda i: (0, 0), **once),
            pl.BlockSpec((tile, columns), lambda i: (i, 0)),
            pl.BlockSpec((tile, columns), lambda i: (i, 0)),
        ],
        out_specs=(pl.BlockSpec((tile, columns), lambda i: (i, 0)), pl.BlockSpec((1, tile), lambda i: (0, i))),
        scratch_shapes=[pltpu.VMEM((rows, columns), jnp.bfloat16)] + [pltpu.VMEM((rows, LANES), jnp.float32)] * 3,
        compiler_params=pltpu.CompilerParams(vmem_limit_bytes=VMEM_LIMIT),
        name="head_update",
    )(rows_all, stats, logits, head_weight, head_ema)


def on_device(parts, ways, hidden, norm_gain, labels, head_weight, head_ema, gain_ema):
    batches, own_rows, features = hidden.shape
    own = batches * own_rows
    count = own * parts
    gain_wide = norm_gain.astype(jnp.float32)
    wide = hidden.reshape(own, features).astype(jnp.float32)
    factor = lax.rsqrt(jnp.mean(wide * wide, axis=-1, keepdims=True) + EPS)
    scaled = (wide * factor * gain_wide).astype(jnp.bfloat16)
    mine = lax.iota(jnp.int32, parts)[:, None] == lax.axis_index("fsdp")
    label_row = jnp.where(mine, labels.reshape(1, own).astype(jnp.float32), 0.0).reshape(1, count)

    rows_all = gather_rows(scaled, parts, ways).reshape(count, features)
    logits, stats = local_logits(rows_all, head_weight, label_row)
    stats = exchange(stats, parts, ways, combine_stats, 1, "exchange_stats")
    head_new, partial_sum = head_update(rows_all, stats, logits, head_weight, head_ema, own)
    gain_grad = exchange(partial_sum, parts, ways, combine_sum, 2, "exchange_gain").reshape(features) / gain_wide
    gain_new = BETA * gain_ema + (1.0 - BETA) * gain_grad * gain_grad / count
    return (head_new, gain_new)


def solution(mesh):
    return jax.shard_map(
        functools.partial(on_device, mesh.shape["fsdp"], mesh.shape["vocab"]),
        mesh=mesh,
        in_specs=(
            P(None, "fsdp", None),
            P(),
            P(None, "fsdp"),
            P(None, ("vocab", "fsdp")),
            P(None, ("vocab", "fsdp")),
            P(),
        ),
        out_specs=(P(None, ("vocab", "fsdp")), P()),
        check_vma=False,
    )
```

```python
import functools

import jax
import jax.numpy as jnp
from jax import lax
from jax.experimental import pallas as pl
from jax.experimental.pallas import tpu as pltpu
from jax.sharding import PartitionSpec as P

BETA = 0.99
EPS = 1e-05
LANES = 128
MESH = pl.DeviceIdType.MESH
VMEM_LIMIT = 60 * 1024 * 1024


def normalize_kernel(hidden_ref, gain_ref, scaled_ref):
    wide = hidden_ref[...].astype(jnp.float32)
    factor = lax.rsqrt(jnp.mean(wide * wide, axis=-1, keepdims=True) + EPS)
    scaled_ref[...] = (wide * factor * gain_ref[...].astype(jnp.float32)).astype(jnp.bfloat16)


def bits_of(size):
    return [1 << place for place in reversed(range(size.bit_length() - 1))]


def flip(index, mask):
    for place in range(mask.bit_length()):
        bit = 1 << place
        if mask & bit:
            index = index + bit - 2 * bit * lax.rem(lax.div(index, bit), 2)
    return index


def shared_width(features, ways):
    return features // 8 // LANES * LANES if ways == 4 else 0


def gather_sends(parts, ways, features):
    return (parts - 1) * (ways + (2 if shared_width(features, ways) else 0))


def gather_kernel(parts, ways, own_ref, all_ref, send_sem, recv_sem, local_sem):
    part, way = lax.axis_index("fsdp"), lax.axis_index("vocab")
    features = own_ref.shape[1]
    both = shared_width(features, ways)
    single = (features - 2 * both) // ways
    part_bits, way_bits = bits_of(parts), bits_of(ways)

    barrier = pltpu.get_barrier_semaphore()
    for bit in part_bits:
        pl.semaphore_signal(barrier, inc=1, device_id=(way, flip(part, bit)), device_id_type=MESH)
    for bit in way_bits:
        pl.semaphore_signal(barrier, inc=1, device_id=(flip(way, bit), part), device_id_type=MESH)
    pl.semaphore_wait(barrier, len(part_bits) + len(way_bits))

    kinds = ([("both", [1])] if both else []) + [("single", way_bits)]

    def columns(kind, piece_mask):
        piece = flip(way, piece_mask)
        if kind == "both":
            return pl.ds(pl.multiple_of(single * ways + lax.rem(piece, 2) * both, LANES), both)
        return pl.ds(pl.multiple_of(piece * single, LANES), single)

    def slot(kind, part_mask, piece_mask):
        return (part_mask - 1) * (ways + 2) + (ways if kind == "both" else 0) + piece_mask

    sends = []

    def send(kind, part_mask, piece_mask, part_bit, way_bit):
        where = columns(kind, piece_mask)
        shard = flip(part, part_mask)
        target = all_ref.at[shard, :, where]
        copy = pltpu.make_async_remote_copy(
            src_ref=target if part_mask else own_ref.at[:, where],
            dst_ref=target,
            send_sem=send_sem.at[len(sends)],
            recv_sem=recv_sem.at[slot(kind, part_mask ^ part_bit, piece_mask ^ way_bit)],
            device_id=(flip(way, way_bit), flip(part, part_bit)),
            device_id_type=MESH,
        )
        copy.start()
        sends.append(copy)

    def forward(kind, kind_bits, part_mask, piece_mask):
        if not piece_mask:
            for bit in part_bits:
                if not part_mask or bit < part_mask & -part_mask:
                    send(kind, part_mask, 0, bit, 0)
        if part_mask:
            for bit in kind_bits:
                if not piece_mask or bit < piece_mask & -piece_mask:
                    send(kind, part_mask, piece_mask, 0, bit)

    def arrive(kind, part_mask, piece_mask):
        target = all_ref.at[flip(part, part_mask), :, columns(kind, piece_mask)]
        pltpu.make_async_remote_copy(
            src_ref=target,
            dst_ref=target,
            send_sem=send_sem.at[0],
            recv_sem=recv_sem.at[slot(kind, part_mask, piece_mask)],
            device_id=(flip(way, way_bits[-1]), part),
            device_id_type=MESH,
        ).wait_recv()

    keep = pltpu.make_async_copy(own_ref, all_ref.at[part], local_sem)
    for kind, kind_bits in reversed(kinds):
        forward(kind, kind_bits, 0, 0)
    keep.start()
    order = sorted(range(1, parts), key=lambda mask: (mask.bit_count(), -mask))
    for part_mask in order:
        for kind, kind_bits in reversed(kinds):
            arrive(kind, part_mask, 0)
            forward(kind, kind_bits, part_mask, 0)
    for last in (False, True):
        for part_mask in order:
            for kind, kind_bits in reversed(kinds):
                for piece_mask in range(1, 2 * kind_bits[0]):
                    if (piece_mask % 2 == 1) == last:
                        arrive(kind, part_mask, piece_mask)
                        forward(kind, kind_bits, part_mask, piece_mask)
    for copy in sends:
        copy.wait_send()
    keep.wait()


def gather_rows(own, parts, ways):
    rows, features = own.shape
    sends = gather_sends(parts, ways, features)
    return pl.pallas_call(
        functools.partial(gather_kernel, parts, ways),
        out_shape=jax.ShapeDtypeStruct((parts, rows, features), own.dtype),
        in_specs=[pl.BlockSpec(memory_space=pltpu.VMEM)],
        out_specs=pl.BlockSpec(memory_space=pl.ANY),
        scratch_shapes=[
            pltpu.SemaphoreType.DMA((sends,)),
            pltpu.SemaphoreType.DMA(((parts - 1) * (ways + 2),)),
            pltpu.SemaphoreType.DMA,
        ],
        compiler_params=pltpu.CompilerParams(collective_id=0, has_side_effects=True),
        name="gather_rows",
    )(own)


def exchange_kernel(parts, ways, combine, x_ref, y_ref, part_slots, way_slots, half, send_sem, part_sem, way_sem):
    part, way = lax.axis_index("fsdp"), lax.axis_index("vocab")
    barrier = pltpu.get_barrier_semaphore()
    for step in range(1, parts):
        pl.semaphore_signal(barrier, inc=1, device_id=(way, lax.rem(part + step, parts)), device_id_type=MESH)
    for step in range(1, ways):
        pl.semaphore_signal(barrier, inc=1, device_id=(lax.rem(way + step, ways), part), device_id_type=MESH)
    pl.semaphore_wait(barrier, parts + ways - 2)

    copies = []
    for step in range(1, parts):
        copies.append(
            pltpu.make_async_remote_copy(
                src_ref=x_ref,
                dst_ref=part_slots.at[part],
                send_sem=send_sem.at[step - 1],
                recv_sem=part_sem.at[step - 1],
                device_id=(way, lax.rem(part + step, parts)),
                device_id_type=MESH,
            )
        )
        copies[-1].start()
    part_slots[part] = x_ref[...]
    for step in range(1, parts):
        pltpu.make_async_remote_copy(
            src_ref=x_ref,
            dst_ref=part_slots.at[lax.rem(part + parts - step, parts)],
            send_sem=send_sem.at[step - 1],
            recv_sem=part_sem.at[step - 1],
            device_id=(way, lax.rem(part + step, parts)),
            device_id_type=MESH,
        ).wait_recv()
    half[...] = combine([part_slots[index] for index in range(parts)], False)
    for step in range(1, ways):
        copies.append(
            pltpu.make_async_remote_copy(
                src_ref=half,
                dst_ref=way_slots.at[way],
                send_sem=send_sem.at[parts - 2 + step],
                recv_sem=way_sem.at[step - 1],
                device_id=(lax.rem(way + step, ways), part),
                device_id_type=MESH,
            )
        )
        copies[-1].start()
    way_slots[way] = half[...]
    for step in range(1, ways):
        pltpu.make_async_remote_copy(
            src_ref=half,
            dst_ref=way_slots.at[lax.rem(way + ways - step, ways)],
            send_sem=send_sem.at[parts - 2 + step],
            recv_sem=way_sem.at[step - 1],
            device_id=(lax.rem(way + step, ways), part),
            device_id_type=MESH,
        ).wait_recv()
    y_ref[...] = combine([way_slots[index] for index in range(ways)], True)
    for copy in copies:
        copy.wait_send()


def exchange(x, parts, ways, combine, number, name):
    return pl.pallas_call(
        functools.partial(exchange_kernel, parts, ways, combine),
        out_shape=jax.ShapeDtypeStruct(x.shape, x.dtype),
        in_specs=[pl.BlockSpec(memory_space=pltpu.VMEM)],
        out_specs=pl.BlockSpec(memory_space=pltpu.VMEM),
        scratch_shapes=[
            pltpu.VMEM((parts,) + x.shape, x.dtype),
            pltpu.VMEM((ways,) + x.shape, x.dtype),
            pltpu.VMEM(x.shape, x.dtype),
            pltpu.SemaphoreType.DMA((parts + ways - 2,)),
            pltpu.SemaphoreType.DMA((parts - 1,)),
            pltpu.SemaphoreType.DMA((ways - 1,)),
        ],
        compiler_params=pltpu.CompilerParams(collective_id=number, has_side_effects=True),
        name=name,
    )(x)


def combine_stats(terms, labels_done):
    top = functools.reduce(jnp.maximum, [term[0:1] for term in terms])
    total = sum(term[1:2] * jnp.exp(term[0:1] - top) for term in terms)
    label = terms[0][2:3] if labels_done else sum(term[2:3] for term in terms)
    return jnp.concatenate([top, total, label, jnp.zeros((1, top.shape[1]), jnp.float32)], axis=0)


def combine_sum(terms, labels_done):
    return sum(terms)


def logits_kernel(rows_ref, weight_ref, label_ref, logits_ref, stats_ref, top_ref, total_ref):
    step = pl.program_id(0)

    @pl.when(step == 0)
    def _():
        top_ref[...] = jnp.full_like(top_ref, -jnp.inf)
        total_ref[...] = jnp.zeros_like(total_ref)

    logits_ref[...] = jnp.dot(rows_ref[...], weight_ref[...], preferred_element_type=jnp.float32)
    groups = [logits_ref[:, start : start + LANES] for start in range(0, logits_ref.shape[1], LANES)]
    old = top_ref[...]
    top = functools.reduce(jnp.maximum, groups, old)
    total_ref[...] = total_ref[...] * jnp.exp(old - top) + sum(jnp.exp(group - top) for group in groups)
    top_ref[...] = top

    @pl.when(step == pl.num_programs(0) - 1)
    def _():
        wide_top = top_ref[...].T
        row_top = jnp.max(wide_top, axis=0, keepdims=True)
        row_total = jnp.sum(total_ref[...].T * jnp.exp(wide_top - row_top), axis=0, keepdims=True)
        stats_ref[...] = jnp.concatenate(
            [row_top, row_total, label_ref[...], jnp.zeros((1, row_top.shape[1]), jnp.float32)], axis=0
        )


def local_logits(rows_all, head_weight, label_row):
    rows, features = rows_all.shape
    columns = head_weight.shape[1]
    tile = min(256, columns)
    return pl.pallas_call(
        logits_kernel,
        grid=(columns // tile,),
        out_shape=(
            jax.ShapeDtypeStruct((rows, columns), jnp.float32),
            jax.ShapeDtypeStruct((4, rows), jnp.float32),
        ),
        in_specs=[
            pl.BlockSpec((rows, features), lambda i: (0, 0), pipeline_mode=pl.Buffered(1)),
            pl.BlockSpec((features, tile), lambda i: (0, i)),
            pl.BlockSpec((1, rows), lambda i: (0, 0)),
        ],
        out_specs=(pl.BlockSpec((rows, tile), lambda i: (0, i)), pl.BlockSpec((4, rows), lambda i: (0, 0))),
        scratch_shapes=[pltpu.VMEM((rows, LANES), jnp.float32)] * 2,
        compiler_params=pltpu.CompilerParams(vmem_limit_bytes=VMEM_LIMIT),
        name="local_logits",
    )(rows_all, head_weight, label_row)


def update_kernel(
    chunk, rows_ref, stats_ref, logits_ref, weight_ref, ema_ref, new_ref, gain_ref, slope_ref, top_ref, scale_ref, label_ref
):
    count, columns = logits_ref.shape

    @pl.when(pl.program_id(0) == 0)
    def _():
        stats = stats_ref[...]
        top_ref[...] = jnp.broadcast_to(stats[0:1], (LANES, count)).T
        scale_ref[...] = jnp.broadcast_to(1.0 / stats[1:2], (LANES, count)).T
        label_ref[...] = jnp.broadcast_to(stats[2:3], (LANES, count)).T
        first = (lax.axis_index("vocab") * lax.axis_size("fsdp") + lax.axis_index("fsdp")) * columns

        @pl.loop(0, count // chunk)
        def _(index):
            some = pl.ds(pl.multiple_of(index * chunk, chunk), chunk)
            top, scale, label = top_ref[some, :], scale_ref[some, :], label_ref[some, :].astype(jnp.int32)
            label = label - first
            lane = lax.broadcasted_iota(jnp.int32, (chunk, LANES), 1)
            for start in range(0, columns, LANES):
                chances = jnp.exp(logits_ref[some, start : start + LANES] - top) * scale
                hits = (label == lane + start).astype(jnp.float32)
                slope_ref[some, start : start + LANES] = (chances - hits).astype(slope_ref.dtype)

    mix = (1.0 - BETA) / count
    tall = rows_ref[...].T
    total = jnp.zeros((tall.shape[0], LANES), jnp.float32)
    width = min(512, columns)
    for start in range(0, columns, width):
        gradient = jnp.dot(tall, slope_ref[:, start : start + width], preferred_element_type=jnp.float32)
        new_ref[:, start : start + width] = BETA * ema_ref[:, start : start + width] + mix * gradient * gradient
        product = weight_ref[:, start : start + width].astype(jnp.float32) * gradient
        for lane in range(0, width, LANES):
            total = total + product[:, lane : lane + LANES]
    gain_ref[...] = jnp.sum(total.T, axis=0, keepdims=True)


def head_update(rows_all, stats, logits, head_weight, head_ema, chunk):
    rows, features = rows_all.shape
    columns = head_weight.shape[1]
    tile = 512 if features % 512 == 0 else 256
    once = dict(pipeline_mode=pl.Buffered(1))
    return pl.pallas_call(
        functools.partial(update_kernel, chunk),
        grid=(features // tile,),
        out_shape=(
            jax.ShapeDtypeStruct((features, columns), jnp.float32),
            jax.ShapeDtypeStruct((1, features), jnp.float32),
        ),
        in_specs=[
            pl.BlockSpec((rows, tile), lambda i: (0, i)),
            pl.BlockSpec((4, rows), lambda i: (0, 0)),
            pl.BlockSpec((rows, columns), lambda i: (0, 0), **once),
            pl.BlockSpec((tile, columns), lambda i: (i, 0)),
            pl.BlockSpec((tile, columns), lambda i: (i, 0)),
        ],
        out_specs=(pl.BlockSpec((tile, columns), lambda i: (i, 0)), pl.BlockSpec((1, tile), lambda i: (0, i))),
        scratch_shapes=[pltpu.VMEM((rows, columns), jnp.bfloat16)] + [pltpu.VMEM((rows, LANES), jnp.float32)] * 3,
        compiler_params=pltpu.CompilerParams(vmem_limit_bytes=VMEM_LIMIT),
        name="head_update",
    )(rows_all, stats, logits, head_weight, head_ema)


def on_device(parts, ways, hidden, norm_gain, labels, head_weight, head_ema, gain_ema):
    batches, own_rows, features = hidden.shape
    own = batches * own_rows
    count = own * parts
    gain_wide = norm_gain.astype(jnp.float32)
    scaled = pl.pallas_call(
        normalize_kernel,
        out_shape=jax.ShapeDtypeStruct((own, features), jnp.bfloat16),
        name="normalize",
    )(hidden.reshape(own, features), norm_gain.reshape(1, features))
    mine = lax.iota(jnp.int32, parts)[:, None] == lax.axis_index("fsdp")
    label_row = jnp.where(mine, labels.reshape(1, own).astype(jnp.float32), 0.0).reshape(1, count)

    rows_all = gather_rows(scaled, parts, ways).reshape(count, features)
    logits, stats = local_logits(rows_all, head_weight, label_row)
    stats = exchange(stats, parts, ways, combine_stats, 1, "exchange_stats")
    head_new, partial_sum = head_update(rows_all, stats, logits, head_weight, head_ema, own)
    gain_grad = exchange(partial_sum, parts, ways, combine_sum, 2, "exchange_gain").reshape(features) / gain_wide
    gain_new = BETA * gain_ema + (1.0 - BETA) * gain_grad * gain_grad / count
    return (head_new, gain_new)


def solution(mesh):
    return jax.shard_map(
        functools.partial(on_device, mesh.shape["fsdp"], mesh.shape["vocab"]),
        mesh=mesh,
        in_specs=(
            P(None, "fsdp", None),
            P(),
            P(None, "fsdp"),
            P(None, ("vocab", "fsdp")),
            P(None, ("vocab", "fsdp")),
            P(),
        ),
        out_specs=(P(None, ("vocab", "fsdp")), P()),
        check_vma=False,
    )
```
